512 devices in a mesh: lat: 64 (over z, x), mem: 8 (over y, core).
Axes of the slice: x: 4, y: 4, z: 16, core: 2. Of those that a mesh axis runs over, the one named last changes fastest.
Arguments:
- obs_rows: float32 [262144, 32], P(('lat', 'mem')), may hold values from -0.18 to 0.18
- obs_band: int32 [262144, 1], P(('lat', 'mem')), may hold values from 0 to 63; in each aligned block of 512 rows (0 to 511, 512 to 1023, ...) at most 32 rows name the same one
- obs_cell: int32 [262144], P(('lat', 'mem')), may hold values from 0 to 1439
- obs_top: int32 [262144], P(('lat', 'mem')), may hold values from 1 to 32
- perturb: bfloat16 [64, 1440, 1024], P('lat', None, 'mem'), may hold values from -6 to 6
- control: bfloat16 [64, 1440, 1024], P('lat', None, 'mem'), may hold values from -6 to 6
Outputs:
- gradient: float32 [64, 1440, 1024], P('lat', None, 'mem')
The draws below stay inside these ranges and needn't reach their ends.
Inputs may be any that keep to these rules, and one draw needn't show every extreme that they name: `obs_band`: the 512 profiles of one device name one band each; no band is named by more than 32 profiles of one device. `obs_cell`: row within the band times 1440 plus the longitude column. `obs_top`: levels below this index carry the profile; the rest are unused.
All inputs are finite; a program needn't handle non-finite values.
Results may differ from the reference program's by a relative error of at most 0.0003.
Values sent between devices are 32-bit elements; how exact they have to be, the bound alone decides.
No kernel may reach another device: no remote copies, remote signals or barrier semaphores. Data moves between devices by JAX's collectives and lax.ppermute only.
A program may use at most 64 MiB of HBM per device.

```python
import math
import jax
import jax.numpy as jnp
import numpy as np
from jax import lax

LAT_DEV = 1
LON = 1440
LEV = 32
OBS_DEV = 512
CAP = 32
NLAT = 64
MEMBERS = 32
OBS = 262144
N_LAT = 64


def place_ends(result, stream_key, low, top_value):
    extent = result.shape
    place = [jax.random.randint(jax.random.fold_in(stream_key, axis), (), 0, extent[axis]) for axis in range(len(extent))]
    result = result.at[tuple(place)].set(low)
    longest = extent.index(max(extent))
    place[longest] = (place[longest] + 1) % extent[longest]
    return result.at[tuple(place)].set(top_value)


def levels(rng, dims, shards, smallest, top_value):
    level = 1.0
    for dim, parts in shards:
        draws = jax.random.uniform(jax.random.fold_in(jax.random.fold_in(rng, 6), dim), (parts,), jnp.float32, smallest / len(shards), top_value / len(shards))
        level = level * jnp.repeat(jnp.exp(draws), dims[dim] // parts).reshape((-1,) + (1,) * (len(dims) - 1 - dim))
    return level


def shared_out(rng, own, number, rows, count, top, limit, slope):
    order = jax.random.permutation(rng, count)
    heavy_load, ordinary = shares(count, rows * top, limit, slope, True), shares(count, rows * top, limit, slope, False)
    places = jnp.arange(count)

    def named(lengths, rotation):
        used = int((lengths > 0).sum())
        fixed = max(1, used // 4)
        passed = fixed + (places - fixed + rotation * (used - fixed)) % max(1, count - fixed)
        return jnp.zeros((count,), jnp.int32).at[order[jnp.where(places < fixed, places, passed)]].set(jnp.asarray(lengths, jnp.int32))

    lengths = jnp.where(number % 4 == 0, named(heavy_load, number // 4), named(ordinary, number - number // 4 - 1))
    mixed = jax.random.permutation(jax.random.fold_in(own, 3), count)
    source_of, sink = mixed[0:count // 2 * 2:2], mixed[1:count // 2 * 2:2]
    margin = jnp.minimum(lengths[source_of] - 1, limit - lengths[sink]) // 2
    margin = jnp.where((source_of == order[0]) | (sink == order[0]) | (lengths[sink] == 0), 0, jnp.maximum(margin, 0))
    passed = jax.random.randint(jax.random.fold_in(own, 4), (count // 2,), 0, 1 << 20) % (margin + 1)
    lengths = lengths.at[source_of].add(-passed).at[sink].add(passed)
    items = jnp.searchsorted(jnp.cumsum(lengths), jnp.arange(rows * top), side="right").astype(jnp.int32)
    listing = items.reshape(top, rows).T
    listing = listing[jax.random.permutation(jax.random.fold_in(own, 1), rows)]
    rotation = jax.random.randint(jax.random.fold_in(own, 2), (rows, 1), 0, top)
    return jnp.take_along_axis(listing, (jnp.arange(top)[None, :] + rotation) % top, axis=1)


def shares(amount, total, bound, slope, full):
    weights = [(1 << 20) // math.isqrt(standing ** slope) + 1 for standing in range(1, amount + 1)]
    largest = bound if full else min(bound, max(-(-total // amount), total * weights[0] // sum(weights)))
    least = 1 if total - largest >= amount - 1 else 0
    counts, spare = [largest] + [least] * (amount - 1), total - largest - least * (amount - 1)
    while spare > 0:
        movable = [i for i in range(1, amount) if counts[i] < largest] or [i for i in range(1, amount) if counts[i] < bound]
        pool, budget = sum([weights[i] for i in movable]), spare
        for i in movable:
            extra = min(bound - counts[i], max(1, budget * weights[i] // pool), spare)
            counts[i] = counts[i] + extra
            spare = spare - extra
    return np.array(counts)


def noise(rng, extent, width, limit, shards=(), held_as=jnp.bfloat16):
    result = width * jax.random.normal(rng, extent, jnp.float32)
    if shards:
        result = result * levels(rng, extent, shards, -0.22, 0.18)
    return jnp.clip(result, -limit, limit).astype(held_as)


def setup_inputs(seed: int = 0) -> dict:
    arg_keys = jax.random.split(jax.random.key(seed), 7)
    obs_rows = noise(arg_keys[0], (OBS, LEV), 0.03, 0.18, ((0, 512),), jnp.float32)
    obs_band_keys = jax.random.split(jax.random.fold_in(arg_keys[1], 1), OBS // OBS_DEV)
    obs_band_turns = jax.random.permutation(jax.random.fold_in(arg_keys[1], 3), OBS // OBS_DEV)
    obs_band = jax.vmap(lambda own, number: shared_out(jax.random.fold_in(arg_keys[1], 2), own, number, OBS_DEV, N_LAT, 1, CAP, 2))(obs_band_keys, obs_band_turns).reshape((OBS, 1))
    obs_cell = place_ends(jax.random.randint(arg_keys[2], (OBS,), 0, LAT_DEV * LON), jax.random.fold_in(arg_keys[2], 1), 0, (LAT_DEV * LON) - 1).astype(jnp.int32)
    obs_top = place_ends(jax.random.randint(arg_keys[3], (OBS,), 1, LEV + 1), jax.random.fold_in(arg_keys[3], 1), 1, LEV).astype(jnp.int32)
    perturb = noise(arg_keys[4], (NLAT, LON, MEMBERS * LEV), 1.0, 6.0, ((0, 64), (2, 8)))
    control = noise(arg_keys[5], (NLAT, LON, MEMBERS * LEV), 1.0, 6.0, ((0, 64), (2, 8)))
    return dict(obs_rows=obs_rows, obs_band=obs_band, obs_cell=obs_cell, obs_top=obs_top, perturb=perturb, control=control)


def kernel(count, spread, periodic):
    positions = jnp.arange(count, dtype=jnp.float32)
    distance = jnp.abs(positions[:, None] - positions[None, :])
    if periodic:
        distance = jnp.minimum(distance, count - distance)
    return jnp.exp(-0.5 * (distance / spread) ** 2)


def lon_spread(row, all_rows, lon_count):
    base = float(max(lon_count // 60, 4))
    latitude = 1.2 * (row.astype(jnp.float32) + 0.5) / all_rows
    return base / jnp.cos(latitude)


def reference(obs_rows, obs_band, obs_cell, obs_top, perturb, control):
    level_ids = jnp.arange(LEV, dtype=jnp.int32)
    level_mask = (level_ids[None, :] < obs_top[:, None]).astype(jnp.float32)
    profiles = obs_rows * level_mask
    flat_index = (obs_band[:, 0] * (LAT_DEV * LON) + obs_cell).astype(jnp.int32)
    innovation = jnp.zeros((NLAT * LON, LEV), jnp.float32).at[flat_index].add(profiles)
    innovation = innovation.reshape(NLAT, LON, LEV)
    vert = kernel(LEV, 1.0, False)
    latk = kernel(NLAT, 8.0 * LAT_DEV, False)
    members_view = perturb.reshape(NLAT, LON, MEMBERS, LEV)

    def member_field(member):
        slab = lax.dynamic_index_in_dim(members_view, member, 2, keepdims=False).astype(jnp.float32)
        product = slab * innovation
        vertical = jnp.einsum('ml,rjl->rjm', vert, product, precision=lax.Precision.HIGHEST)
        return jnp.einsum('rR,Rjm->rjm', latk, vertical, precision=lax.Precision.HIGHEST)

    fields = lax.map(member_field, jnp.arange(MEMBERS, dtype=jnp.int32))

    def row_field(row):
        lonk = kernel(LON, lon_spread(row, NLAT, LON), True)
        data = lax.dynamic_index_in_dim(fields, row, 1, keepdims=False)
        smoothed = jnp.einsum('jJ,kJl->jkl', lonk, data, precision=lax.Precision.HIGHEST)
        return smoothed.reshape(LON, MEMBERS * LEV)

    zonal = lax.map(row_field, jnp.arange(NLAT, dtype=jnp.int32))
    return control.astype(jnp.float32) + zonal
```

```python
import functools

import jax
import jax.numpy as jnp
from jax import lax
from jax.experimental import pallas as pl
from jax.experimental.pallas import tpu as pltpu
from jax.sharding import PartitionSpec as P

CAP = 32
F32 = jnp.float32
BF16 = jnp.bfloat16
PARAMS = pltpu.CompilerParams(vmem_limit_bytes=48 * 1024 * 1024)


def split3(x):
    high = x.astype(BF16)
    rest = x - high.astype(F32)
    mid = rest.astype(BF16)
    low = (rest - mid.astype(F32)).astype(BF16)
    return high, mid, low


def split2(x):
    high = x.astype(BF16)
    return high, (x - high.astype(F32)).astype(BF16)


def dot(a, b, dims=((1,), (0,))):
    return lax.dot_general(a, b, (dims, ((), ())), preferred_element_type=F32)


def bucket_kernel(rows_ref, band_ref, cell_ref, top_ref, out_ref, bands):
    count, levels = rows_ref.shape
    band, cell, top = band_ref[...], cell_ref[...], top_ref[...]
    owner = (lax.broadcasted_iota(jnp.int32, (bands, count), 0) == band).astype(F32)
    owner_b = owner.astype(BF16)
    before = (
        lax.broadcasted_iota(jnp.int32, (count, count), 0)
        < lax.broadcasted_iota(jnp.int32, (count, count), 1)
    ).astype(F32).astype(BF16)
    earlier = dot(owner_b, before)
    rank = jnp.sum(earlier * owner, axis=0, keepdims=True).astype(jnp.int32)
    kept = lax.broadcasted_iota(jnp.int32, (levels, count), 0) < top
    values = jnp.where(kept, jnp.transpose(rows_ref[...]), 0.0)
    parts = split3(values)
    for slot in range(0, CAP, 4):
        total = None
        for part in parts:
            chosen = jnp.concatenate(
                [jnp.where(rank == slot + k, part.astype(F32), 0.0) for k in range(4)], axis=0
            ).astype(BF16)
            term = dot(owner_b, chosen, ((1,), (1,)))
            total = term if total is None else total + term
        out_ref[:, slot * levels : (slot + 4) * levels] = total
    cells = jnp.where(
        lax.broadcasted_iota(jnp.int32, (128, count), 0) == rank, cell.astype(F32), 0.0
    )
    high, low = split2(cells)
    out_ref[:, CAP * levels :] = dot(owner_b, high, ((1,), (1,))) + dot(
        owner_b, low, ((1,), (1,))
    )


def bucket(rows, band, cell, top, bands):
    count, levels = rows.shape
    return pl.pallas_call(
        functools.partial(bucket_kernel, bands=bands),
        out_shape=jax.ShapeDtypeStruct((bands, CAP * levels + 128), F32),
        compiler_params=PARAMS,
        name="bucket",
    )(rows, band.reshape(1, count), cell.reshape(1, count), top.reshape(1, count))


def deposit_kernel(got_ref, out_ref, levels):
    sources = got_ref.shape[0]
    groups, per_group, cells = out_ref.shape
    got = got_ref[...]
    width = 256 // sources
    acc = jnp.zeros((3 * levels, cells), F32)
    places = lax.broadcasted_iota(jnp.int32, (256, cells), 1).astype(F32)
    for first in range(0, CAP, width):
        block = jnp.transpose(got[:, first * levels : (first + width) * levels])
        values = jnp.concatenate(
            [block[k * levels : (k + 1) * levels] for k in range(width)], axis=1
        )
        parts = jnp.concatenate(split3(values), axis=0)
        base = CAP * levels + first
        where = jnp.concatenate([got[:, base + k : base + k + 1] for k in range(width)], axis=0)
        hits = jnp.where(places == where, 1.0, 0.0).astype(BF16)
        acc = acc + dot(parts, hits)
    grid = acc[:levels] + acc[levels : 2 * levels] + acc[2 * levels :]
    for group in range(groups):
        out_ref[group] = grid[group * per_group : (group + 1) * per_group]


def deposit(got, levels, groups, cells):
    return pl.pallas_call(
        functools.partial(deposit_kernel, levels=levels),
        out_shape=jax.ShapeDtypeStruct((groups, levels // groups, cells), F32),
        compiler_params=PARAMS,
        name="deposit",
    )(got)


def product_kernel(perturb_ref, innovation_ref, out_ref, levels):
    columns = perturb_ref.shape[1]
    groups, per_group, cells = innovation_ref.shape
    innovation = jnp.concatenate([innovation_ref[g] for g in range(groups)], axis=0)
    parts = jnp.concatenate(split3(innovation), axis=0)
    spread = (
        lax.broadcasted_iota(jnp.int32, (3 * levels, columns), 0) % levels
        == lax.broadcasted_iota(jnp.int32, (3 * levels, columns), 1) % levels
    ).astype(F32).astype(BF16)
    on_columns = dot(parts, spread, ((0,), (0,)))
    product = perturb_ref[...].astype(F32) * on_columns
    row = lax.broadcasted_iota(jnp.int32, (columns, columns), 0)
    column = lax.broadcasted_iota(jnp.int32, (columns, columns), 1)
    distance = (row % levels - column % levels).astype(F32)
    vert = jnp.where(row // levels == column // levels, jnp.exp(-0.5 * distance * distance), 0.0)
    vert_high, vert_low = split2(vert)
    high, low = split2(product)
    out_ref[...] = dot(high, vert_high) + (dot(low, vert_high) + dot(high, vert_low))


def product_vertical(perturb, innovation, levels):
    return pl.pallas_call(
        functools.partial(product_kernel, levels=levels),
        out_shape=jax.ShapeDtypeStruct(perturb.shape, F32),
        compiler_params=PARAMS,
        name="product_vertical",
    )(perturb, innovation)


def zonal_kernel(spread_ref, field_ref, control_ref, out_ref, twice, block):
    lon_count, columns = field_ref.shape
    high, low = split2(field_ref[...])
    both = jnp.concatenate([high, low], axis=1)
    twice[0:lon_count] = both
    twice[lon_count : 2 * lon_count] = both
    place = lax.broadcasted_iota(jnp.int32, (block, lon_count), 0)
    other = lax.broadcasted_iota(jnp.int32, (block, lon_count), 1)
    distance = jnp.abs(place - other).astype(F32)
    distance = jnp.minimum(distance, lon_count - distance) / spread_ref[0]
    lonk_high, lonk_low = split2(jnp.exp(-0.5 * distance * distance))
    for first in range(0, lon_count, block):
        window = twice[first : first + lon_count]
        wide = dot(lonk_high, window)
        narrow = dot(lonk_low, window[:, :columns])
        out_ref[first : first + block] = control_ref[first : first + block].astype(F32) + (
            wide[:, :columns] + (wide[:, columns:] + narrow)
        )


def zonal(field, control, spread):
    lon_count, columns = field.shape
    block = 288
    return pl.pallas_call(
        functools.partial(zonal_kernel, block=block),
        out_shape=jax.ShapeDtypeStruct(field.shape, F32),
        in_specs=[
            pl.BlockSpec(memory_space=pltpu.SMEM),
            pl.BlockSpec(memory_space=pltpu.VMEM),
            pl.BlockSpec(memory_space=pltpu.VMEM),
        ],
        scratch_shapes=[pltpu.VMEM((2 * lon_count, 2 * columns), BF16)],
        compiler_params=PARAMS,
        name="zonal",
    )(spread, field, control)


def local(obs_rows, obs_band, obs_cell, obs_top, perturb, control):
    bands, mem = lax.axis_size("lat"), lax.axis_size("mem")
    _, lon_count, columns = perturb.shape
    levels = obs_rows.shape[1]
    send = bucket(obs_rows, obs_band, obs_cell, obs_top, bands)
    got = lax.all_to_all(send, "lat", split_axis=0, concat_axis=0, tiled=True)
    partial_grid = deposit(got, levels, mem, lon_count)
    pieces = lax.all_to_all(partial_grid, "mem", split_axis=0, concat_axis=0, tiled=True)
    piece = jnp.sum(pieces, axis=0, keepdims=True)
    innovation = lax.all_to_all(
        jnp.broadcast_to(piece, pieces.shape), "mem", split_axis=0, concat_axis=0, tiled=True
    )
    vertical = product_vertical(perturb[0], innovation, levels)
    positions = jnp.arange(bands, dtype=F32)
    latk = jnp.exp(-0.5 * ((positions[:, None] - positions[None, :]) / 8.0) ** 2)
    columns_here = lax.all_to_all(
        vertical.reshape(bands, lon_count * columns // bands),
        "lat",
        split_axis=0,
        concat_axis=0,
        tiled=True,
    )
    smoothed = jnp.dot(latk, columns_here, precision=lax.Precision.HIGHEST)
    returned = lax.all_to_all(smoothed, "lat", split_axis=0, concat_axis=0, tiled=True)
    latitude = 1.2 * (lax.axis_index("lat").astype(F32) + 0.5) / bands
    spread = float(max(lon_count // 60, 4)) / jnp.cos(latitude)
    result = zonal(returned.reshape(lon_count, columns), control[0], spread.reshape(1))
    return result[None]


def solution(mesh):
    return jax.shard_map(
        local,
        mesh=mesh,
        in_specs=(
            P(("lat", "mem"), None),
            P(("lat", "mem"), None),
            P(("lat", "mem")),
            P(("lat", "mem")),
            P("lat", None, "mem"),
            P("lat", None, "mem"),
        ),
        out_specs=P("lat", None, "mem"),
        check_vma=False,
    )
```

```python
import functools

import jax
import jax.numpy as jnp
from jax import lax
from jax.experimental import pallas as pl
from jax.experimental.pallas import tpu as pltpu
from jax.sharding import PartitionSpec as P

CAP = 32
F32 = jnp.float32
BF16 = jnp.bfloat16
PARAMS = pltpu.CompilerParams(vmem_limit_bytes=48 * 1024 * 1024)


def split3(x):
    high = x.astype(BF16)
    rest = x - high.astype(F32)
    mid = rest.astype(BF16)
    low = (rest - mid.astype(F32)).astype(BF16)
    return high, mid, low


def split2(x):
    high = x.astype(BF16)
    return high, (x - high.astype(F32)).astype(BF16)


def dot(a, b, dims=((1,), (0,))):
    return lax.dot_general(a, b, (dims, ((), ())), preferred_element_type=F32)


def bucket_kernel(rows_ref, band_ref, cell_ref, top_ref, out_ref, bands):
    levels, count = rows_ref.shape
    band, cell, top = band_ref[...], cell_ref[...], top_ref[...]
    owner = (lax.broadcasted_iota(jnp.int32, (bands, count), 0) == band).astype(F32)
    owner_b = owner.astype(BF16)
    before = (
        lax.broadcasted_iota(jnp.int32, (count, count), 0)
        < lax.broadcasted_iota(jnp.int32, (count, count), 1)
    ).astype(F32).astype(BF16)
    earlier = dot(owner_b, before)
    rank = jnp.sum(earlier * owner, axis=0, keepdims=True).astype(jnp.int32)
    kept = lax.broadcasted_iota(jnp.int32, (levels, count), 0) < top
    values = jnp.where(kept, rows_ref[...], 0.0)
    parts = split3(values)
    for slot in range(0, CAP, 4):
        total = None
        for part in parts:
            chosen = jnp.concatenate(
                [jnp.where(rank == slot + k, part.astype(F32), 0.0) for k in range(4)], axis=0
            ).astype(BF16)
            term = dot(owner_b, chosen, ((1,), (1,)))
            total = term if total is None else total + term
        out_ref[:, slot * levels : (slot + 4) * levels] = total
    cells = jnp.where(
        lax.broadcasted_iota(jnp.int32, (128, count), 0) == rank, cell.astype(F32), 0.0
    )
    high, low = split2(cells)
    out_ref[:, CAP * levels :] = dot(owner_b, high, ((1,), (1,))) + dot(
        owner_b, low, ((1,), (1,))
    )


def bucket(rows, band, cell, top, bands):
    count, levels = rows.shape
    return pl.pallas_call(
        functools.partial(bucket_kernel, bands=bands),
        out_shape=jax.ShapeDtypeStruct((bands, CAP * levels + 128), F32),
        compiler_params=PARAMS,
        name="bucket",
    )(rows.T, band.reshape(1, count), cell.reshape(1, count), top.reshape(1, count))


def deposit_kernel(core_ref, got_ref, mine_ref, other_ref):
    sources = got_ref.shape[0]
    half, cells = mine_ref.shape
    levels = 2 * half
    got = got_ref[...]
    width = 256 // sources
    acc = jnp.zeros((3 * levels, cells), F32)
    places = lax.broadcasted_iota(jnp.int32, (256, cells), 1).astype(F32)
    for first in range(0, CAP, width):
        block = jnp.transpose(got[:, first * levels : (first + width) * levels])
        values = jnp.concatenate(
            [block[k * levels : (k + 1) * levels] for k in range(width)], axis=1
        )
        parts = jnp.concatenate(split3(values), axis=0)
        base = CAP * levels + first
        where = jnp.concatenate([got[:, base + k : base + k + 1] for k in range(width)], axis=0)
        hits = jnp.where(places == where, 1.0, 0.0).astype(BF16)
        acc = acc + dot(parts, hits)
    grid = acc[:levels] + acc[levels : 2 * levels] + acc[2 * levels :]
    first_core = core_ref[0] == 0
    mine_ref[...] = jnp.where(first_core, grid[:half], grid[half:])
    other_ref[...] = jnp.where(first_core, grid[half:], grid[:half])


def deposit(core, got, levels, cells):
    half = jax.ShapeDtypeStruct((levels // 2, cells), F32)
    return pl.pallas_call(
        deposit_kernel,
        out_shape=(half, half),
        in_specs=[
            pl.BlockSpec(memory_space=pltpu.SMEM),
            pl.BlockSpec(memory_space=pltpu.VMEM),
        ],
        compiler_params=PARAMS,
        name="deposit",
    )(core, got)


def product_kernel(core_ref, perturb_ref, mine_ref, other_ref, out_ref):
    cells, columns = perturb_ref.shape
    levels = 2 * mine_ref.shape[0]
    first_core = core_ref[0] == 0
    mine, other = mine_ref[...], other_ref[...]
    innovation = jnp.concatenate(
        [jnp.where(first_core, mine, other), jnp.where(first_core, other, mine)], axis=0
    )
    parts = jnp.concatenate(split3(innovation), axis=0)
    spread = (
        lax.broadcasted_iota(jnp.int32, (3 * levels, columns), 0) % levels
        == lax.broadcasted_iota(jnp.int32, (3 * levels, columns), 1) % levels
    ).astype(F32).astype(BF16)
    on_columns = dot(parts, spread, ((0,), (0,)))
    product = perturb_ref[...].astype(F32) * on_columns
    row = lax.broadcasted_iota(jnp.int32, (columns, columns), 0)
    column = lax.broadcasted_iota(jnp.int32, (columns, columns), 1)
    distance = (row % levels - column % levels).astype(F32)
    vert = jnp.where(row // levels == column // levels, jnp.exp(-0.5 * distance * distance), 0.0)
    vert_high, vert_low = split2(vert)
    high, low = split2(product)
    out_ref[:cells] = dot(high, vert_high) + (dot(low, vert_high) + dot(high, vert_low))
    out_ref[cells:] = jnp.zeros((out_ref.shape[0] - cells, columns), F32)


def product_vertical(core, perturb, mine, other, rows):
    return pl.pallas_call(
        product_kernel,
        out_shape=jax.ShapeDtypeStruct((rows, perturb.shape[1]), F32),
        in_specs=[pl.BlockSpec(memory_space=pltpu.SMEM)]
        + [pl.BlockSpec(memory_space=pltpu.VMEM)] * 3,
        compiler_params=PARAMS,
        name="product_vertical",
    )(core, perturb, mine, other)


def meridional_kernel(field_ref, out_ref, bands):
    each = field_ref.shape[0] // bands
    row = lax.broadcasted_iota(jnp.int32, (bands, bands), 0)
    column = lax.broadcasted_iota(jnp.int32, (bands, bands), 1)
    distance = (row - column).astype(F32) / 8.0
    high, low = split2(jnp.exp(-0.5 * distance * distance))
    weights = jnp.concatenate([high, high, low], axis=1)
    for place in range(each):
        rows = pl.ds(place, bands, stride=each)
        field_high, field_low = split2(field_ref[rows, :])
        out_ref[rows, :] = dot(
            weights, jnp.concatenate([field_high, field_low, field_high], axis=0)
        )


def meridional(field, bands):
    return pl.pallas_call(
        functools.partial(meridional_kernel, bands=bands),
        out_shape=jax.ShapeDtypeStruct(field.shape, F32),
        compiler_params=PARAMS,
        name="meridional",
    )(field)


def reach_kernel(spread_ref, high_ref, low_ref):
    block, lon_count = high_ref.shape
    place = lax.broadcasted_iota(jnp.int32, (block, lon_count), 0)
    other = lax.broadcasted_iota(jnp.int32, (block, lon_count), 1)
    distance = jnp.abs(place - other).astype(F32)
    distance = jnp.minimum(distance, lon_count - distance) / spread_ref[0]
    high_ref[...], low_ref[...] = split2(jnp.exp(-0.5 * distance * distance))


def reach(spread, block, lon_count):
    part = jax.ShapeDtypeStruct((block, lon_count), BF16)
    return pl.pallas_call(
        reach_kernel,
        out_shape=(part, part),
        in_specs=[pl.BlockSpec(memory_space=pltpu.SMEM)],
        compiler_params=PARAMS,
        cost_estimate=pl.CostEstimate(
            flops=20 * block * lon_count,
            transcendentals=block * lon_count,
            bytes_accessed=4 * block * lon_count,
        ),
        name="reach",
    )(spread)


def zonal_kernel(high_ref, low_ref, field_ref, control_ref, out_ref, twice):
    lon_count, columns = control_ref.shape
    block = high_ref.shape[0]
    high, low = split2(field_ref[:lon_count])
    both = jnp.concatenate([high, low], axis=1)
    twice[0:lon_count] = both
    twice[lon_count : 2 * lon_count] = both
    for first in range(0, lon_count, block):
        window = twice[first : first + lon_count]
        wide = dot(high_ref[...], window)
        narrow = dot(low_ref[...], window[:, :columns])
        out_ref[first : first + block] = control_ref[first : first + block].astype(F32) + (
            wide[:, :columns] + (wide[:, columns:] + narrow)
        )


def zonal(high, low, field, control):
    lon_count, columns = control.shape
    return pl.pallas_call(
        zonal_kernel,
        out_shape=jax.ShapeDtypeStruct(control.shape, F32),
        scratch_shapes=[pltpu.VMEM((2 * lon_count, 2 * columns), BF16)],
        compiler_params=PARAMS,
        name="zonal",
    )(high, low, field, control)


def local(obs_rows, obs_band, obs_cell, obs_top, perturb, control):
    bands, mem = lax.axis_size("lat"), lax.axis_size("mem")
    _, lon_count, columns = perturb.shape
    levels = obs_rows.shape[1]
    index = lax.axis_index("mem")
    core = (index % 2).astype(jnp.int32).reshape(1)

    def swap(x, flip):
        return lax.ppermute(x, "mem", [(m, m ^ flip) for m in range(mem)])

    send = bucket(obs_rows, obs_band, obs_cell, obs_top, bands)
    got = lax.all_to_all(send, "lat", split_axis=0, concat_axis=0, tiled=True)
    mine, other = deposit(core, got, levels, lon_count)
    mine = mine + swap(other, 1)
    mine = mine + swap(mine, 2)
    mine = mine + swap(mine, 6)
    other = swap(mine, 1)
    each = -(-lon_count // bands)
    padded = each * bands

    def transpose(field):
        pieces = field.reshape(bands, 1, each * columns)
        pieces = lax.all_to_all(pieces, "lat", split_axis=0, concat_axis=0, tiled=True)
        return pieces.reshape(padded, columns)

    vertical = product_vertical(core, perturb[0], mine, other, padded)
    smoothed = meridional(transpose(vertical), bands)
    returned = transpose(smoothed)
    latitude = 1.2 * (lax.axis_index("lat").astype(F32) + 0.5) / bands
    spread = float(max(lon_count // 60, 4)) / jnp.cos(latitude)
    high, low = reach(spread.reshape(1), lon_count // 5, lon_count)
    return zonal(high, low, returned, control[0])[None]


def solution(mesh):
    return jax.shard_map(
        local,
        mesh=mesh,
        in_specs=(
            P(("lat", "mem"), None),
            P(("lat", "mem"), None),
            P(("lat", "mem")),
            P(("lat", "mem")),
            P("lat", None, "mem"),
            P("lat", None, "mem"),
        ),
        out_specs=P("lat", None, "mem"),
        check_vma=False,
    )
```

```python
import functools

import jax
import jax.numpy as jnp
from jax import lax
from jax.experimental import pallas as pl
from jax.experimental.pallas import tpu as pltpu
from jax.sharding import Mesh, PartitionSpec as P

CAP = 32
F32 = jnp.float32
BF16 = jnp.bfloat16
PARAMS = pltpu.CompilerParams(vmem_limit_bytes=20 * 1024 * 1024)


def split3(x):
    high = x.astype(BF16)
    rest = x - high.astype(F32)
    mid = rest.astype(BF16)
    low = (rest - mid.astype(F32)).astype(BF16)
    return high, mid, low


def split2(x):
    high = x.astype(BF16)
    return high, (x - high.astype(F32)).astype(BF16)


def dot(a, b, dims=((1,), (0,))):
    return lax.dot_general(a, b, (dims, ((), ())), preferred_element_type=F32)


def bucket_kernel(
    rows_any, band_any, cell_any, top_any, out_ref, rows_ref, band_ref, cell_ref, top_ref, sems
):
    levels, count = rows_ref.shape
    bands = out_ref.shape[0] * out_ref.shape[1] // (CAP * levels + 128)
    stride = out_ref.shape[0] // bands
    copies = [
        pltpu.make_async_copy(source, target, sems.at[k])
        for k, (source, target) in enumerate(
            [
                (band_any, band_ref),
                (cell_any, cell_ref),
                (top_any, top_ref),
                (rows_any, rows_ref),
            ]
        )
    ]
    for copy in copies:
        copy.start()
    before = (
        lax.broadcasted_iota(jnp.int32, (count, count), 0)
        < lax.broadcasted_iota(jnp.int32, (count, count), 1)
    ).astype(F32).astype(BF16)
    copies[0].wait()
    owner = (lax.broadcasted_iota(jnp.int32, (bands, count), 0) == band_ref[...]).astype(F32)
    owner_b = owner.astype(BF16)
    earlier = dot(owner_b, before)
    rank = jnp.sum(earlier * owner, axis=0, keepdims=True).astype(jnp.int32)
    for copy in copies[1:]:
        copy.wait()
    kept = lax.broadcasted_iota(jnp.int32, (levels, count), 0) < top_ref[...]
    parts = [part.astype(F32) for part in split3(jnp.where(kept, rows_ref[...], 0.0))]
    for place in range(stride - 1):
        total = None
        for part in parts:
            chosen = jnp.concatenate(
                [jnp.where(rank == 4 * place + k, part, 0.0) for k in range(4)], axis=0
            ).astype(BF16)
            term = dot(owner_b, chosen, ((1,), (1,)))
            total = term if total is None else total + term
        out_ref[pl.ds(place, bands, stride=stride), :] = total
    cells = jnp.where(
        lax.broadcasted_iota(jnp.int32, (128, count), 0) == rank, cell_ref[...].astype(F32), 0.0
    )
    high, low = split2(cells)
    out_ref[pl.ds(stride - 1, bands, stride=stride), :] = dot(
        owner_b, high, ((1,), (1,))
    ) + dot(owner_b, low, ((1,), (1,)))


def bucket(rows, band, cell, top, bands):
    count, levels = rows.shape
    row = pltpu.VMEM((1, count), jnp.int32)
    return pl.pallas_call(
        bucket_kernel,
        out_shape=jax.ShapeDtypeStruct((bands * (CAP * levels // 128 + 1), 128), F32),
        in_specs=[pl.BlockSpec(memory_space=pltpu.HBM)] * 4,
        scratch_shapes=[
            pltpu.VMEM((levels, count), F32),
            row,
            row,
            row,
            pltpu.SemaphoreType.DMA((4,)),
        ],
        compiler_params=PARAMS,
        name="bucket",
    )(
        *(
            pltpu.with_memory_space_constraint(x, pltpu.HBM)
            for x in (
                rows.T,
                band.reshape(1, count),
                cell.reshape(1, count),
                top.reshape(1, count),
            )
        )
    )


def deposit_kernel(got_ref, out_ref, levels):
    groups, per_group, cells = out_ref.shape
    width = 128 // levels
    stride = CAP // width + 1
    sources = got_ref.shape[0] // stride
    spots = got_ref[pl.ds(stride - 1, sources, stride=stride), :]
    acc = jnp.zeros((3 * levels, cells), F32)
    places = lax.broadcasted_iota(jnp.int32, (width * sources, cells), 1).astype(F32)
    for place in range(stride - 1):
        block = jnp.transpose(got_ref[pl.ds(place, sources, stride=stride), :])
        values = jnp.concatenate(
            [block[k * levels : (k + 1) * levels] for k in range(width)], axis=1
        )
        parts = jnp.concatenate(split3(values), axis=0)
        base = place * width
        where = jnp.concatenate([spots[:, base + k : base + k + 1] for k in range(width)], axis=0)
        hits = jnp.where(places == where, 1.0, 0.0).astype(BF16)
        acc = acc + dot(parts, hits)
    grid = acc[:levels] + acc[levels : 2 * levels] + acc[2 * levels :]
    for group in range(groups):
        out_ref[group] = grid[group * per_group : (group + 1) * per_group]


def deposit(got, levels, groups, cells):
    return pl.pallas_call(
        functools.partial(deposit_kernel, levels=levels),
        out_shape=jax.ShapeDtypeStruct((groups, levels // groups, cells), F32),
        compiler_params=PARAMS,
        name="deposit",
    )(got)


def product_kernel(perturb_ref, innovation_ref, out_ref):
    cells, columns = perturb_ref.shape
    groups, per_group, _ = innovation_ref.shape
    levels = groups * per_group
    innovation = jnp.concatenate([innovation_ref[g] for g in range(groups)], axis=0)
    parts = jnp.concatenate(split3(innovation), axis=0)
    spread = (
        lax.broadcasted_iota(jnp.int32, (3 * levels, columns), 0) % levels
        == lax.broadcasted_iota(jnp.int32, (3 * levels, columns), 1) % levels
    ).astype(F32).astype(BF16)
    on_columns = dot(parts, spread, ((0,), (0,)))
    product = perturb_ref[...].astype(F32) * on_columns
    row = lax.broadcasted_iota(jnp.int32, (columns, columns), 0)
    column = lax.broadcasted_iota(jnp.int32, (columns, columns), 1)
    distance = (row % levels - column % levels).astype(F32)
    vert = jnp.where(row // levels == column // levels, jnp.exp(-0.5 * distance * distance), 0.0)
    vert_high, vert_low = split2(vert)
    high, low = split2(product)
    out_ref[:cells] = dot(high, vert_high) + (dot(low, vert_high) + dot(high, vert_low))
    out_ref[cells:] = jnp.zeros((out_ref.shape[0] - cells, columns), F32)


def product_vertical(perturb, innovation, rows):
    return pl.pallas_call(
        product_kernel,
        out_shape=jax.ShapeDtypeStruct((rows, perturb.shape[1]), F32),
        compiler_params=PARAMS,
        name="product_vertical",
    )(perturb, innovation)


def meridional_kernel(field_ref, out_ref, bands):
    each = field_ref.shape[0] // bands
    row = lax.broadcasted_iota(jnp.int32, (bands, bands), 0)
    column = lax.broadcasted_iota(jnp.int32, (bands, bands), 1)
    distance = (row - column).astype(F32) / 8.0
    high, low = split2(jnp.exp(-0.5 * distance * distance))
    weights = jnp.concatenate([high, high, low], axis=1)
    for place in range(0, each, 2):
        places = [pl.ds(p, bands, stride=each) for p in range(place, min(place + 2, each))]
        taken = jnp.concatenate([field_ref[rows, :] for rows in places], axis=1)
        field_high, field_low = split2(taken)
        mixed = dot(weights, jnp.concatenate([field_high, field_low, field_high], axis=0))
        for k, rows in enumerate(places):
            out_ref[rows, :] = mixed[:, 128 * k : 128 * (k + 1)]


def meridional(field, bands):
    return pl.pallas_call(
        functools.partial(meridional_kernel, bands=bands),
        out_shape=jax.ShapeDtypeStruct(field.shape, F32),
        compiler_params=PARAMS,
        name="meridional",
    )(field)


def reach_kernel(spread_ref, high_ref, low_ref):
    block, lon_count = high_ref.shape
    place = lax.broadcasted_iota(jnp.int32, (block, lon_count), 0)
    other = lax.broadcasted_iota(jnp.int32, (block, lon_count), 1)
    distance = jnp.abs(place - other).astype(F32)
    distance = jnp.minimum(distance, lon_count - distance) / spread_ref[0]
    high_ref[...], low_ref[...] = split2(jnp.exp(-0.5 * distance * distance))


def reach(spread, block, lon_count):
    part = jax.ShapeDtypeStruct((block, lon_count), BF16)
    return pl.pallas_call(
        reach_kernel,
        out_shape=(part, part),
        in_specs=[pl.BlockSpec(memory_space=pltpu.SMEM)],
        compiler_params=PARAMS,
        cost_estimate=pl.CostEstimate(
            flops=20 * block * lon_count,
            transcendentals=block * lon_count,
            bytes_accessed=4 * block * lon_count,
        ),
        name="reach",
    )(spread)


def zonal_kernel(high_ref, low_ref, field_ref, control_ref, out_ref, twice):
    lon_count, columns = control_ref.shape
    block = high_ref.shape[0]
    high, low = split2(field_ref[:lon_count])
    both = jnp.concatenate([high, low], axis=1)
    twice[0:lon_count] = both
    twice[lon_count : 2 * lon_count] = both
    for first in range(0, lon_count, block):
        window = twice[first : first + lon_count]
        wide = dot(high_ref[...], window)
        narrow = dot(low_ref[...], window[:, :columns])
        out_ref[first : first + block] = control_ref[first : first + block].astype(F32) + (
            wide[:, :columns] + (wide[:, columns:] + narrow)
        )


def zonal(high, low, field, control):
    lon_count, columns = control.shape
    return pl.pallas_call(
        zonal_kernel,
        out_shape=jax.ShapeDtypeStruct(control.shape, F32),
        scratch_shapes=[pltpu.VMEM((2 * lon_count, 2 * columns), BF16)],
        compiler_params=PARAMS,
        name="zonal",
    )(high, low, field, control)


def local(obs_rows, obs_band, obs_cell, obs_top, perturb, control):
    bands = lax.axis_size("lat")
    mem = lax.axis_size("core") * lax.axis_size("y")
    _, lon_count, columns = perturb.shape
    levels = obs_rows.shape[1]

    def exchange(pieces, axes):
        return lax.all_to_all(pieces, axes, split_axis=0, concat_axis=0, tiled=True)

    send = bucket(obs_rows, obs_band, obs_cell, obs_top, bands)
    got = exchange(send.reshape(bands, 1, -1), "lat").reshape(send.shape)
    pieces = exchange(deposit(got, levels, mem, lon_count), ("core", "y"))
    piece = jnp.sum(pieces, axis=0, keepdims=True)
    innovation = exchange(jnp.broadcast_to(piece, pieces.shape), ("core", "y"))
    each = -(-lon_count // bands)
    padded = each * bands

    def transpose(field):
        pieces = field.reshape(bands, 1, each * columns)
        return exchange(pieces, "lat").reshape(padded, columns)

    vertical = product_vertical(perturb[0], innovation, padded)
    smoothed = meridional(transpose(vertical), bands)
    returned = transpose(smoothed)
    latitude = 1.2 * (lax.axis_index("lat").astype(F32) + 0.5) / bands
    spread = float(max(lon_count // 60, 4)) / jnp.cos(latitude)
    high, low = reach(spread.reshape(1), lon_count // 5, lon_count)
    return zonal(high, low, returned, control[0])[None]


def solution(mesh):
    bands, mem = mesh.shape["lat"], mesh.shape["mem"]
    finer = Mesh(mesh.devices.reshape(bands, mem // 2, 2), ("lat", "y", "core"))
    everything, members = ("lat", "y", "core"), ("y", "core")
    return jax.shard_map(
        local,
        mesh=finer,
        in_specs=(
            P(everything, None),
            P(everything, None),
            P(everything),
            P(everything),
            P("lat", None, members),
            P("lat", None, members),
        ),
        out_specs=P("lat", None, members),
        check_vma=False,
    )
```

```python
import functools

import jax
import jax.numpy as jnp
from jax import lax
from jax.experimental import pallas as pl
from jax.experimental.pallas import tpu as pltpu
from jax.sharding import Mesh, PartitionSpec as P

CAP = 32
F32 = jnp.float32
BF16 = jnp.bfloat16
PARAMS = pltpu.CompilerParams(vmem_limit_bytes=20 * 1024 * 1024)


def split3(x):
    high = x.astype(BF16)
    rest = x - high.astype(F32)
    mid = rest.astype(BF16)
    low = (rest - mid.astype(F32)).astype(BF16)
    return high, mid, low


def split2(x):
    high = x.astype(BF16)
    return high, (x - high.astype(F32)).astype(BF16)


def dot(a, b, dims=((1,), (0,))):
    return lax.dot_general(a, b, (dims, ((), ())), preferred_element_type=F32)


def bucket_kernel(
    rows_any, band_any, cell_any, top_any, out_ref, rows_ref, band_ref, cell_ref, top_ref, sems
):
    levels, count = rows_ref.shape
    bands = out_ref.shape[0] * out_ref.shape[1] // (CAP * levels + 128)
    stride = out_ref.shape[0] // bands
    copies = [
        pltpu.make_async_copy(source, target, sems.at[k])
        for k, (source, target) in enumerate(
            [
                (band_any, band_ref),
                (cell_any, cell_ref),
                (top_any, top_ref),
                (rows_any, rows_ref),
            ]
        )
    ]
    for copy in copies:
        copy.start()
    before = (
        lax.broadcasted_iota(jnp.int32, (count, count), 0)
        < lax.broadcasted_iota(jnp.int32, (count, count), 1)
    ).astype(F32).astype(BF16)
    copies[0].wait()
    owner = (lax.broadcasted_iota(jnp.int32, (bands, count), 0) == band_ref[...]).astype(F32)
    owner_b = owner.astype(BF16)
    earlier = dot(owner_b, before)
    rank = jnp.sum(earlier * owner, axis=0, keepdims=True).astype(jnp.int32)
    for copy in copies[1:]:
        copy.wait()
    kept = lax.broadcasted_iota(jnp.int32, (levels, count), 0) < top_ref[...]
    parts = [part.astype(F32) for part in split3(jnp.where(kept, rows_ref[...], 0.0))]
    for place in range(stride - 1):
        total = None
        for part in parts:
            chosen = jnp.concatenate(
                [jnp.where(rank == 4 * place + k, part, 0.0) for k in range(4)], axis=0
            ).astype(BF16)
            term = dot(owner_b, chosen, ((1,), (1,)))
            total = term if total is None else total + term
        out_ref[pl.ds(place, bands, stride=stride), :] = total
    cells = jnp.where(
        lax.broadcasted_iota(jnp.int32, (128, count), 0) == rank, cell_ref[...].astype(F32), 0.0
    )
    high, low = split2(cells)
    out_ref[pl.ds(stride - 1, bands, stride=stride), :] = dot(
        owner_b, high, ((1,), (1,))
    ) + dot(owner_b, low, ((1,), (1,)))


def bucket(rows, band, cell, top, bands):
    count, levels = rows.shape
    row = pltpu.VMEM((1, count), jnp.int32)
    return pl.pallas_call(
        bucket_kernel,
        out_shape=jax.ShapeDtypeStruct((bands * (CAP * levels // 128 + 1), 128), F32),
        in_specs=[pl.BlockSpec(memory_space=pltpu.HBM)] * 4,
        scratch_shapes=[
            pltpu.VMEM((levels, count), F32),
            row,
            row,
            row,
            pltpu.SemaphoreType.DMA((4,)),
        ],
        compiler_params=PARAMS,
        name="bucket",
    )(
        *(
            pltpu.with_memory_space_constraint(x, pltpu.HBM)
            for x in (
                rows.T,
                band.reshape(1, count),
                cell.reshape(1, count),
                top.reshape(1, count),
            )
        )
    )


def deposit_kernel(got_ref, out_ref, levels):
    groups, per_group, cells = out_ref.shape
    width = 128 // levels
    stride = CAP // width + 1
    sources = got_ref.shape[0] // stride
    spots = got_ref[pl.ds(stride - 1, sources, stride=stride), :]
    acc = jnp.zeros((3 * levels, cells), F32)
    places = lax.broadcasted_iota(jnp.int32, (width * sources, cells), 1).astype(F32)
    for place in range(stride - 1):
        block = jnp.transpose(got_ref[pl.ds(place, sources, stride=stride), :])
        values = jnp.concatenate(
            [block[k * levels : (k + 1) * levels] for k in range(width)], axis=1
        )
        parts = jnp.concatenate(split3(values), axis=0)
        base = place * width
        where = jnp.concatenate([spots[:, base + k : base + k + 1] for k in range(width)], axis=0)
        hits = jnp.where(places == where, 1.0, 0.0).astype(BF16)
        acc = acc + dot(parts, hits)
    grid = acc[:levels] + acc[levels : 2 * levels] + acc[2 * levels :]
    for group in range(groups):
        out_ref[group] = grid[group * per_group : (group + 1) * per_group]


def deposit(got, levels, groups, cells):
    return pl.pallas_call(
        functools.partial(deposit_kernel, levels=levels),
        out_shape=jax.ShapeDtypeStruct((groups, levels // groups, cells), F32),
        compiler_params=PARAMS,
        name="deposit",
    )(got)


def product_kernel(turn_ref, perturb_ref, innovation_ref, out_ref):
    del turn_ref
    cells, columns = perturb_ref.shape
    groups, per_group, _ = innovation_ref.shape
    levels = groups * per_group
    innovation = jnp.concatenate([innovation_ref[g] for g in range(groups)], axis=0)
    parts = jnp.concatenate(split3(innovation), axis=0)
    spread = (
        lax.broadcasted_iota(jnp.int32, (3 * levels, columns), 0) % levels
        == lax.broadcasted_iota(jnp.int32, (3 * levels, columns), 1) % levels
    ).astype(F32).astype(BF16)
    on_columns = dot(parts, spread, ((0,), (0,)))
    product = perturb_ref[...].astype(F32) * on_columns
    row = lax.broadcasted_iota(jnp.int32, (columns, columns), 0)
    column = lax.broadcasted_iota(jnp.int32, (columns, columns), 1)
    distance = (row % levels - column % levels).astype(F32)
    vert = jnp.where(row // levels == column // levels, jnp.exp(-0.5 * distance * distance), 0.0)
    vert_high, vert_low = split2(vert)
    high, low = split2(product)
    out_ref[:cells] = dot(high, vert_high) + (dot(low, vert_high) + dot(high, vert_low))
    out_ref[cells:] = jnp.zeros((out_ref.shape[0] - cells, columns), F32)


def product_vertical(turn, perturb, innovation, rows):
    return pl.pallas_call(
        product_kernel,
        out_shape=jax.ShapeDtypeStruct((rows, perturb.shape[1]), F32),
        compiler_params=PARAMS,
        name="product_vertical",
    )(turn, perturb, innovation)


def meridional_kernel(field_ref, out_ref, bands):
    each = field_ref.shape[0] // bands
    row = lax.broadcasted_iota(jnp.int32, (bands, bands), 0)
    column = lax.broadcasted_iota(jnp.int32, (bands, bands), 1)
    distance = (row - column).astype(F32) / 8.0
    high, low = split2(jnp.exp(-0.5 * distance * distance))
    weights = jnp.concatenate([high, high, low], axis=1)
    for place in range(0, each, 2):
        places = [pl.ds(p, bands, stride=each) for p in range(place, min(place + 2, each))]
        taken = jnp.concatenate([field_ref[rows, :] for rows in places], axis=1)
        field_high, field_low = split2(taken)
        mixed = dot(weights, jnp.concatenate([field_high, field_low, field_high], axis=0))
        for k, rows in enumerate(places):
            out_ref[rows, :] = mixed[:, 128 * k : 128 * (k + 1)]


def meridional(field, bands):
    return pl.pallas_call(
        functools.partial(meridional_kernel, bands=bands),
        out_shape=jax.ShapeDtypeStruct(field.shape, F32),
        compiler_params=PARAMS,
        name="meridional",
    )(field)


def reach_kernel(spread_ref, high_ref, low_ref):
    block, lon_count = high_ref.shape
    place = lax.broadcasted_iota(jnp.int32, (block, lon_count), 0)
    other = lax.broadcasted_iota(jnp.int32, (block, lon_count), 1)
    distance = jnp.abs(place - other).astype(F32)
    distance = jnp.minimum(distance, lon_count - distance) / spread_ref[0]
    high_ref[...], low_ref[...] = split2(jnp.exp(-0.5 * distance * distance))


def reach(spread, block, lon_count):
    part = jax.ShapeDtypeStruct((block, lon_count), BF16)
    return pl.pallas_call(
        reach_kernel,
        out_shape=(part, part),
        in_specs=[pl.BlockSpec(memory_space=pltpu.SMEM)],
        compiler_params=PARAMS,
        cost_estimate=pl.CostEstimate(
            flops=20 * block * lon_count,
            transcendentals=block * lon_count,
            bytes_accessed=4 * block * lon_count,
        ),
        name="reach",
    )(spread)


def zonal_kernel(high_ref, low_ref, field_ref, control_ref, out_ref, twice):
    lon_count, columns = control_ref.shape
    block = high_ref.shape[0]
    high, low = split2(field_ref[:lon_count])
    both = jnp.concatenate([high, low], axis=1)
    twice[0:lon_count] = both
    twice[lon_count : 2 * lon_count] = both
    for first in range(0, lon_count, block):
        window = twice[first : first + lon_count]
        wide = dot(high_ref[...], window)
        narrow = dot(low_ref[...], window[:, :columns])
        out_ref[first : first + block] = control_ref[first : first + block].astype(F32) + (
            wide[:, :columns] + (wide[:, columns:] + narrow)
        )


def zonal(high, low, field, control):
    lon_count, columns = control.shape
    return pl.pallas_call(
        zonal_kernel,
        out_shape=jax.ShapeDtypeStruct(control.shape, F32),
        scratch_shapes=[pltpu.VMEM((2 * lon_count, 2 * columns), BF16)],
        compiler_params=PARAMS,
        name="zonal",
    )(high, low, field, control)


def local(obs_rows, obs_band, obs_cell, obs_top, perturb, control):
    bands = lax.axis_size("lat")
    mem = lax.axis_size("core") * lax.axis_size("y")
    _, lon_count, columns = perturb.shape
    levels = obs_rows.shape[1]

    def exchange(pieces, axes):
        return lax.all_to_all(pieces, axes, split_axis=0, concat_axis=0, tiled=True)

    send = bucket(obs_rows, obs_band, obs_cell, obs_top, bands)
    got = exchange(send.reshape(bands, 1, -1), "lat").reshape(send.shape)
    pieces = exchange(deposit(got, levels, mem, lon_count), ("core", "y"))
    piece = jnp.sum(pieces, axis=0, keepdims=True)
    innovation = exchange(jnp.broadcast_to(piece, pieces.shape), ("core", "y"))
    each = -(-lon_count // bands)
    padded = each * bands

    def transpose(field):
        pieces = field.reshape(bands, 1, each * columns)
        return exchange(pieces, "lat").reshape(padded, columns)

    rings = lax.axis_size("y")
    second = [(2 * y + 1, 2 * ((y + 1) % rings) + 1) for y in range(rings)]
    turn = innovation[0, :, :128]
    for _ in range(4):
        turn = lax.ppermute(turn, ("y", "core"), second)
    vertical = product_vertical(turn, perturb[0], innovation, padded)
    smoothed = meridional(transpose(vertical), bands)
    returned = transpose(smoothed)
    latitude = 1.2 * (lax.axis_index("lat").astype(F32) + 0.5) / bands
    spread = float(max(lon_count // 60, 4)) / jnp.cos(latitude)
    high, low = reach(spread.reshape(1), lon_count // 5, lon_count)
    return zonal(high, low, returned, control[0])[None]


def solution(mesh):
    bands, mem = mesh.shape["lat"], mesh.shape["mem"]
    finer = Mesh(mesh.devices.reshape(bands, mem // 2, 2), ("lat", "y", "core"))
    everything, members = ("lat", "y", "core"), ("y", "core")
    return jax.shard_map(
        local,
        mesh=finer,
        in_specs=(
            P(everything, None),
            P(everything, None),
            P(everything),
            P(everything),
            P("lat", None, members),
            P("lat", None, members),
        ),
        out_specs=P("lat", None, members),
        check_vma=False,
    )
```

```python
import functools

import jax
import jax.numpy as jnp
from jax import lax
from jax.experimental import pallas as pl
from jax.experimental.pallas import tpu as pltpu
from jax.sharding import Mesh, PartitionSpec as P

CAP = 32
F32 = jnp.float32
BF16 = jnp.bfloat16
PARAMS = pltpu.CompilerParams(vmem_limit_bytes=20 * 1024 * 1024)


def split3(x):
    high = x.astype(BF16)
    rest = x - high.astype(F32)
    mid = rest.astype(BF16)
    low = (rest - mid.astype(F32)).astype(BF16)
    return high, mid, low


def split2(x):
    high = x.astype(BF16)
    return high, (x - high.astype(F32)).astype(BF16)


def dot(a, b, dims=((1,), (0,))):
    return lax.dot_general(a, b, (dims, ((), ())), preferred_element_type=F32)


def bucket_kernel(
    rows_any, band_any, cell_any, top_any, out_ref, rows_ref, band_ref, cell_ref, top_ref, sems
):
    levels, count = rows_ref.shape
    bands = out_ref.shape[0] * out_ref.shape[1] // (CAP * levels + 128)
    stride = out_ref.shape[0] // bands
    copies = [
        pltpu.make_async_copy(source, target, sems.at[k])
        for k, (source, target) in enumerate(
            [
                (band_any, band_ref),
                (cell_any, cell_ref),
                (top_any, top_ref),
                (rows_any, rows_ref),
            ]
        )
    ]
    for copy in copies:
        copy.start()
    before = (
        lax.broadcasted_iota(jnp.int32, (count, count), 0)
        < lax.broadcasted_iota(jnp.int32, (count, count), 1)
    ).astype(F32).astype(BF16)
    copies[0].wait()
    owner = (lax.broadcasted_iota(jnp.int32, (bands, count), 0) == band_ref[...]).astype(F32)
    owner_b = owner.astype(BF16)
    earlier = dot(owner_b, before)
    rank = jnp.sum(earlier * owner, axis=0, keepdims=True).astype(jnp.int32)
    for copy in copies[1:]:
        copy.wait()
    kept = lax.broadcasted_iota(jnp.int32, (levels, count), 0) < top_ref[...]
    parts = [part.astype(F32) for part in split3(jnp.where(kept, rows_ref[...], 0.0))]
    for place in range(stride - 1):
        total = None
        for part in parts:
            chosen = jnp.concatenate(
                [jnp.where(rank == 4 * place + k, part, 0.0) for k in range(4)], axis=0
            ).astype(BF16)
            term = dot(owner_b, chosen, ((1,), (1,)))
            total = term if total is None else total + term
        out_ref[pl.ds(place, bands, stride=stride), :] = total
    cells = jnp.where(
        lax.broadcasted_iota(jnp.int32, (128, count), 0) == rank, cell_ref[...].astype(F32), 0.0
    )
    high, low = split2(cells)
    out_ref[pl.ds(stride - 1, bands, stride=stride), :] = dot(
        owner_b, high, ((1,), (1,))
    ) + dot(owner_b, low, ((1,), (1,)))


def bucket(rows, band, cell, top, bands):
    count, levels = rows.shape
    row = pltpu.VMEM((1, count), jnp.int32)
    return pl.pallas_call(
        bucket_kernel,
        out_shape=jax.ShapeDtypeStruct((bands * (CAP * levels // 128 + 1), 128), F32),
        in_specs=[pl.BlockSpec(memory_space=pltpu.HBM)] * 4,
        scratch_shapes=[
            pltpu.VMEM((levels, count), F32),
            row,
            row,
            row,
            pltpu.SemaphoreType.DMA((4,)),
        ],
        compiler_params=PARAMS,
        name="bucket",
    )(
        *(
            pltpu.with_memory_space_constraint(x, pltpu.HBM)
            for x in (
                rows.T,
                band.reshape(1, count),
                cell.reshape(1, count),
                top.reshape(1, count),
            )
        )
    )


def deposit_kernel(got_ref, out_ref, levels):
    groups, per_group, cells = out_ref.shape
    width = 128 // levels
    stride = CAP // width + 1
    sources = got_ref.shape[0] // stride
    spots = got_ref[pl.ds(stride - 1, sources, stride=stride), :]
    acc = jnp.zeros((3 * levels, cells), F32)
    places = lax.broadcasted_iota(jnp.int32, (width * sources, cells), 1).astype(F32)
    for place in range(stride - 1):
        block = jnp.transpose(got_ref[pl.ds(place, sources, stride=stride), :])
        values = jnp.concatenate(
            [block[k * levels : (k + 1) * levels] for k in range(width)], axis=1
        )
        parts = jnp.concatenate(split3(values), axis=0)
        base = place * width
        where = jnp.concatenate([spots[:, base + k : base + k + 1] for k in range(width)], axis=0)
        hits = jnp.where(places == where, 1.0, 0.0).astype(BF16)
        acc = acc + dot(parts, hits)
    grid = acc[:levels] + acc[levels : 2 * levels] + acc[2 * levels :]
    for group in range(groups):
        out_ref[group] = grid[group * per_group : (group + 1) * per_group]


def deposit(got, levels, groups, cells):
    return pl.pallas_call(
        functools.partial(deposit_kernel, levels=levels),
        out_shape=jax.ShapeDtypeStruct((groups, levels // groups, cells), F32),
        compiler_params=PARAMS,
        name="deposit",
    )(got)


def product_kernel(turn_ref, perturb_ref, innovation_ref, out_ref):
    del turn_ref
    cells, columns = perturb_ref.shape
    groups, per_group, _ = innovation_ref.shape
    levels = groups * per_group
    innovation = jnp.concatenate([innovation_ref[g] for g in range(groups)], axis=0)
    parts = jnp.concatenate(split3(innovation), axis=0)
    spread = (
        lax.broadcasted_iota(jnp.int32, (3 * levels, columns), 0) % levels
        == lax.broadcasted_iota(jnp.int32, (3 * levels, columns), 1) % levels
    ).astype(F32).astype(BF16)
    on_columns = dot(parts, spread, ((0,), (0,)))
    product = perturb_ref[...].astype(F32) * on_columns
    row = lax.broadcasted_iota(jnp.int32, (columns, columns), 0)
    column = lax.broadcasted_iota(jnp.int32, (columns, columns), 1)
    distance = (row % levels - column % levels).astype(F32)
    vert = jnp.where(row // levels == column // levels, jnp.exp(-0.5 * distance * distance), 0.0)
    vert_high, vert_low = split2(vert)
    high, low = split2(product)
    out_ref[:cells] = dot(high, vert_high) + (dot(low, vert_high) + dot(high, vert_low))
    out_ref[cells:] = jnp.zeros((out_ref.shape[0] - cells, columns), F32)


def product_vertical(turn, perturb, innovation, rows):
    return pl.pallas_call(
        product_kernel,
        out_shape=jax.ShapeDtypeStruct((rows, perturb.shape[1]), F32),
        compiler_params=PARAMS,
        name="product_vertical",
    )(turn, perturb, innovation)


def meridional_kernel(field_ref, out_ref, bands):
    each = field_ref.shape[0] // bands
    row = lax.broadcasted_iota(jnp.int32, (bands, bands), 0)
    column = lax.broadcasted_iota(jnp.int32, (bands, bands), 1)
    distance = (row - column).astype(F32) / 8.0
    high, low = split2(jnp.exp(-0.5 * distance * distance))
    weights = jnp.concatenate([high, high, low], axis=1)
    for place in range(0, each, 2):
        places = [pl.ds(p, bands, stride=each) for p in range(place, min(place + 2, each))]
        taken = jnp.concatenate([field_ref[rows, :] for rows in places], axis=1)
        field_high, field_low = split2(taken)
        mixed = dot(weights, jnp.concatenate([field_high, field_low, field_high], axis=0))
        for k, rows in enumerate(places):
            out_ref[rows, :] = mixed[:, 128 * k : 128 * (k + 1)]


def meridional(field, bands):
    return pl.pallas_call(
        functools.partial(meridional_kernel, bands=bands),
        out_shape=jax.ShapeDtypeStruct(field.shape, F32),
        compiler_params=PARAMS,
        name="meridional",
    )(field)


def reach_kernel(spread_ref, high_ref, low_ref):
    block, lon_count = high_ref.shape
    place = lax.broadcasted_iota(jnp.int32, (block, lon_count), 0)
    other = lax.broadcasted_iota(jnp.int32, (block, lon_count), 1)
    distance = jnp.abs(place - other).astype(F32)
    distance = jnp.minimum(distance, lon_count - distance) / spread_ref[0]
    high_ref[...], low_ref[...] = split2(jnp.exp(-0.5 * distance * distance))


def reach(spread, block, lon_count):
    part = jax.ShapeDtypeStruct((block, lon_count), BF16)
    return pl.pallas_call(
        reach_kernel,
        out_shape=(part, part),
        in_specs=[pl.BlockSpec(memory_space=pltpu.SMEM)],
        compiler_params=PARAMS,
        cost_estimate=pl.CostEstimate(
            flops=20 * block * lon_count,
            transcendentals=block * lon_count,
            bytes_accessed=4 * block * lon_count,
        ),
        name="reach",
    )(spread)


def zonal_kernel(high_ref, low_ref, field_ref, control_ref, out_ref, twice):
    lon_count, columns = control_ref.shape
    block = high_ref.shape[0]
    high, low = split2(field_ref[:lon_count])
    both = jnp.concatenate([high, low], axis=1)
    twice[0:lon_count] = both
    twice[lon_count : 2 * lon_count] = both
    starts = list(range(0, lon_count, block))
    for pair in range(0, len(starts), 2):
        windows = [twice[first : first + lon_count] for first in starts[pair : pair + 2]]
        narrow = dot(low_ref[...], jnp.concatenate([w[:, :columns] for w in windows], axis=1))
        for k, window in enumerate(windows):
            wide = dot(high_ref[...], window)
            rows = pl.ds(starts[pair + k], block)
            out_ref[rows] = control_ref[rows].astype(F32) + (
                wide[:, :columns]
                + (wide[:, columns:] + narrow[:, k * columns : (k + 1) * columns])
            )


def zonal(high, low, field, control):
    lon_count, columns = control.shape
    return pl.pallas_call(
        zonal_kernel,
        out_shape=jax.ShapeDtypeStruct(control.shape, F32),
        scratch_shapes=[pltpu.VMEM((2 * lon_count, 2 * columns), BF16)],
        compiler_params=PARAMS,
        name="zonal",
    )(high, low, field, control)


def local(obs_rows, obs_band, obs_cell, obs_top, perturb, control):
    bands = lax.axis_size("lat")
    mem = lax.axis_size("core") * lax.axis_size("y")
    _, lon_count, columns = perturb.shape
    levels = obs_rows.shape[1]

    def exchange(pieces, axes):
        return lax.all_to_all(pieces, axes, split_axis=0, concat_axis=0, tiled=True)

    send = bucket(obs_rows, obs_band, obs_cell, obs_top, bands)
    got = exchange(send.reshape(bands, 1, -1), "lat").reshape(send.shape)
    pieces = exchange(deposit(got, levels, mem, lon_count), ("core", "y"))
    piece = jnp.sum(pieces, axis=0, keepdims=True)
    innovation = exchange(jnp.broadcast_to(piece, pieces.shape), ("core", "y"))
    each = -(-lon_count // bands)
    padded = each * bands

    def transpose(field):
        pieces = field.reshape(bands, 1, each * columns)
        return exchange(pieces, "lat").reshape(padded, columns)

    rings = lax.axis_size("y")
    second = [(2 * y + 1, 2 * ((y + 1) % rings) + 1) for y in range(rings)]
    turn = innovation[:4]
    for _ in range(3):
        turn = lax.ppermute(turn, ("y", "core"), second)
    vertical = product_vertical(turn, perturb[0], innovation, padded)
    smoothed = meridional(transpose(vertical), bands)
    returned = transpose(smoothed)
    latitude = 1.2 * (lax.axis_index("lat").astype(F32) + 0.5) / bands
    spread = float(max(lon_count // 60, 4)) / jnp.cos(latitude)
    high, low = reach(spread.reshape(1), lon_count // 5, lon_count)
    return zonal(high, low, returned, control[0])[None]


def solution(mesh):
    bands, mem = mesh.shape["lat"], mesh.shape["mem"]
    finer = Mesh(mesh.devices.reshape(bands, mem // 2, 2), ("lat", "y", "core"))
    everything, members = ("lat", "y", "core"), ("y", "core")
    return jax.shard_map(
        local,
        mesh=finer,
        in_specs=(
            P(everything, None),
            P(everything, None),
            P(everything),
            P(everything),
            P("lat", None, members),
            P("lat", None, members),
        ),
        out_specs=P("lat", None, members),
        check_vma=False,
    )
```

```python
import functools

import jax
import jax.numpy as jnp
from jax import lax
from jax.experimental import pallas as pl
from jax.experimental.pallas import tpu as pltpu
from jax.sharding import Mesh, PartitionSpec as P

CAP = 32
F32 = jnp.float32
BF16 = jnp.bfloat16
PARAMS = pltpu.CompilerParams(vmem_limit_bytes=20 * 1024 * 1024)


def split3(x):
    high = x.astype(BF16)
    rest = x - high.astype(F32)
    mid = rest.astype(BF16)
    low = (rest - mid.astype(F32)).astype(BF16)
    return high, mid, low


def split2(x):
    high = x.astype(BF16)
    return high, (x - high.astype(F32)).astype(BF16)


def dot(a, b, dims=((1,), (0,))):
    return lax.dot_general(a, b, (dims, ((), ())), preferred_element_type=F32)


def bucket_kernel(
    rows_any, band_any, cell_any, top_any, out_ref, rows_ref, band_ref, cell_ref, top_ref, sems
):
    levels, count = rows_ref.shape
    bands = out_ref.shape[0] * out_ref.shape[1] // (CAP * levels + 128)
    stride = out_ref.shape[0] // bands
    copies = [
        pltpu.make_async_copy(source, target, sems.at[k])
        for k, (source, target) in enumerate(
            [
                (band_any, band_ref),
                (cell_any, cell_ref),
                (top_any, top_ref),
                (rows_any, rows_ref),
            ]
        )
    ]
    for copy in copies:
        copy.start()
    before = (
        lax.broadcasted_iota(jnp.int32, (count, count), 0)
        < lax.broadcasted_iota(jnp.int32, (count, count), 1)
    ).astype(F32).astype(BF16)
    copies[0].wait()
    owner = (lax.broadcasted_iota(jnp.int32, (bands, count), 0) == band_ref[...]).astype(F32)
    owner_b = owner.astype(BF16)
    earlier = dot(owner_b, before)
    rank = jnp.sum(earlier * owner, axis=0, keepdims=True).astype(jnp.int32)
    for copy in copies[1:]:
        copy.wait()
    kept = lax.broadcasted_iota(jnp.int32, (levels, count), 0) < top_ref[...]
    parts = [part.astype(F32) for part in split3(jnp.where(kept, rows_ref[...], 0.0))]
    for place in range(stride - 1):
        total = None
        for part in parts:
            chosen = jnp.concatenate(
                [jnp.where(rank == 4 * place + k, part, 0.0) for k in range(4)], axis=0
            ).astype(BF16)
            term = dot(owner_b, chosen, ((1,), (1,)))
            total = term if total is None else total + term
        out_ref[pl.ds(place, bands, stride=stride), :] = total
    cells = jnp.where(
        lax.broadcasted_iota(jnp.int32, (128, count), 0) == rank, cell_ref[...].astype(F32), 0.0
    )
    high, low = split2(cells)
    out_ref[pl.ds(stride - 1, bands, stride=stride), :] = dot(
        owner_b, high, ((1,), (1,))
    ) + dot(owner_b, low, ((1,), (1,)))


def bucket(rows, band, cell, top, bands):
    count, levels = rows.shape
    row = pltpu.VMEM((1, count), jnp.int32)
    return pl.pallas_call(
        bucket_kernel,
        out_shape=jax.ShapeDtypeStruct((bands * (CAP * levels // 128 + 1), 128), F32),
        in_specs=[pl.BlockSpec(memory_space=pltpu.HBM)] * 4,
        scratch_shapes=[
            pltpu.VMEM((levels, count), F32),
            row,
            row,
            row,
            pltpu.SemaphoreType.DMA((4,)),
        ],
        compiler_params=PARAMS,
        name="bucket",
    )(
        *(
            pltpu.with_memory_space_constraint(x, pltpu.HBM)
            for x in (
                rows.T,
                band.reshape(1, count),
                cell.reshape(1, count),
                top.reshape(1, count),
            )
        )
    )


def deposit_kernel(got_ref, out_ref, levels):
    groups, per_group, cells = out_ref.shape
    width = 128 // levels
    stride = CAP // width + 1
    sources = got_ref.shape[0] // stride
    spots = got_ref[pl.ds(stride - 1, sources, stride=stride), :]
    acc = jnp.zeros((3 * levels, cells), F32)
    places = lax.broadcasted_iota(jnp.int32, (width * sources, cells), 1).astype(F32)
    for place in range(stride - 1):
        block = jnp.transpose(got_ref[pl.ds(place, sources, stride=stride), :])
        values = jnp.concatenate(
            [block[k * levels : (k + 1) * levels] for k in range(width)], axis=1
        )
        parts = jnp.concatenate(split3(values), axis=0)
        base = place * width
        where = jnp.concatenate([spots[:, base + k : base + k + 1] for k in range(width)], axis=0)
        hits = jnp.where(places == where, 1.0, 0.0).astype(BF16)
        acc = acc + dot(parts, hits)
    grid = acc[:levels] + acc[levels : 2 * levels] + acc[2 * levels :]
    for group in range(groups):
        out_ref[group] = grid[group * per_group : (group + 1) * per_group]


def deposit(got, levels, groups, cells):
    return pl.pallas_call(
        functools.partial(deposit_kernel, levels=levels),
        out_shape=jax.ShapeDtypeStruct((groups, levels // groups, cells), F32),
        compiler_params=PARAMS,
        name="deposit",
    )(got)


def product_kernel(turn_ref, perturb_ref, innovation_ref, out_ref):
    del turn_ref
    cells, columns = perturb_ref.shape
    groups, per_group, _ = innovation_ref.shape
    levels = groups * per_group
    innovation = jnp.concatenate([innovation_ref[g] for g in range(groups)], axis=0)
    parts = jnp.concatenate(split3(innovation), axis=0)
    spread = (
        lax.broadcasted_iota(jnp.int32, (3 * levels, columns), 0) % levels
        == lax.broadcasted_iota(jnp.int32, (3 * levels, columns), 1) % levels
    ).astype(F32).astype(BF16)
    on_columns = dot(parts, spread, ((0,), (0,)))
    product = perturb_ref[...].astype(F32) * on_columns
    row = lax.broadcasted_iota(jnp.int32, (columns, columns), 0)
    column = lax.broadcasted_iota(jnp.int32, (columns, columns), 1)
    distance = (row % levels - column % levels).astype(F32)
    vert = jnp.where(row // levels == column // levels, jnp.exp(-0.5 * distance * distance), 0.0)
    vert_high, vert_low = split2(vert)
    high, low = split2(product)
    out_ref[:cells] = dot(high, vert_high) + (dot(low, vert_high) + dot(high, vert_low))
    out_ref[cells:] = jnp.zeros((out_ref.shape[0] - cells, columns), F32)


def product_vertical(turn, perturb, innovation, rows):
    return pl.pallas_call(
        product_kernel,
        out_shape=jax.ShapeDtypeStruct((rows, perturb.shape[1]), F32),
        compiler_params=PARAMS,
        name="product_vertical",
    )(turn, perturb, innovation)


def meridional_kernel(field_ref, out_ref, bands):
    each = field_ref.shape[0] // bands
    row = lax.broadcasted_iota(jnp.int32, (bands, bands), 0)
    column = lax.broadcasted_iota(jnp.int32, (bands, bands), 1)
    distance = (row - column).astype(F32) / 8.0
    high, low = split2(jnp.exp(-0.5 * distance * distance))
    weights = jnp.concatenate([high, high, low], axis=1)
    for place in range(0, each, 2):
        places = [pl.ds(p, bands, stride=each) for p in range(place, min(place + 2, each))]
        taken = jnp.concatenate([field_ref[rows, :] for rows in places], axis=1)
        field_high, field_low = split2(taken)
        mixed = dot(weights, jnp.concatenate([field_high, field_low, field_high], axis=0))
        for k, rows in enumerate(places):
            out_ref[rows, :] = mixed[:, 128 * k : 128 * (k + 1)]


def meridional(field, bands):
    return pl.pallas_call(
        functools.partial(meridional_kernel, bands=bands),
        out_shape=jax.ShapeDtypeStruct(field.shape, F32),
        compiler_params=PARAMS,
        name="meridional",
    )(field)


def reach_kernel(spread_ref, high_ref, low_ref):
    block, lon_count = high_ref.shape
    place = lax.broadcasted_iota(jnp.int32, (block, lon_count), 0)
    other = lax.broadcasted_iota(jnp.int32, (block, lon_count), 1)
    distance = jnp.abs(place - other).astype(F32)
    distance = jnp.minimum(distance, lon_count - distance) / spread_ref[0]
    high_ref[...], low_ref[...] = split2(jnp.exp(-0.5 * distance * distance))


def reach(spread, block, lon_count):
    part = jax.ShapeDtypeStruct((block, lon_count), BF16)
    return pl.pallas_call(
        reach_kernel,
        out_shape=(part, part),
        in_specs=[pl.BlockSpec(memory_space=pltpu.SMEM)],
        compiler_params=PARAMS,
        cost_estimate=pl.CostEstimate(
            flops=20 * block * lon_count,
            transcendentals=block * lon_count,
            bytes_accessed=4 * block * lon_count,
        ),
        name="reach",
    )(spread)


def zonal_kernel(high_ref, low_ref, field_ref, control_ref, out_ref, twice):
    lon_count, columns = control_ref.shape
    block = high_ref.shape[0]
    high, low = split2(field_ref[:lon_count])
    both = jnp.concatenate([high, low], axis=1)
    twice[0:lon_count] = both
    twice[lon_count : 2 * lon_count] = both
    starts = list(range(0, lon_count, block))
    for pair in range(0, len(starts), 2):
        windows = [twice[first : first + lon_count] for first in starts[pair : pair + 2]]
        narrow = dot(low_ref[...], jnp.concatenate([w[:, :columns] for w in windows], axis=1))
        for k, window in enumerate(windows):
            wide = dot(high_ref[...], window)
            rows = pl.ds(starts[pair + k], block)
            out_ref[rows] = control_ref[rows].astype(F32) + (
                wide[:, :columns]
                + (wide[:, columns:] + narrow[:, k * columns : (k + 1) * columns])
            )


def zonal(high, low, field, control):
    lon_count, columns = control.shape
    return pl.pallas_call(
        zonal_kernel,
        out_shape=jax.ShapeDtypeStruct(control.shape, F32),
        scratch_shapes=[pltpu.VMEM((2 * lon_count, 2 * columns), BF16)],
        compiler_params=PARAMS,
        name="zonal",
    )(high, low, field, control)


def local(obs_rows, obs_band, obs_cell, obs_top, perturb, control):
    bands = lax.axis_size("lat")
    mem = lax.axis_size("core") * lax.axis_size("y")
    _, lon_count, columns = perturb.shape
    levels = obs_rows.shape[1]

    def exchange(pieces, axes):
        return lax.all_to_all(pieces, axes, split_axis=0, concat_axis=0, tiled=True)

    send = bucket(obs_rows, obs_band, obs_cell, obs_top, bands)
    got = exchange(send.reshape(bands, 1, -1), "lat").reshape(send.shape)
    pieces = exchange(deposit(got, levels, mem, lon_count), ("core", "y"))
    piece = jnp.sum(pieces, axis=0, keepdims=True)
    innovation = exchange(jnp.broadcast_to(piece, pieces.shape), ("core", "y"))
    each = -(-lon_count // bands)
    padded = each * bands

    def transpose(field):
        pieces = field.reshape(bands, 1, each * columns)
        return exchange(pieces, "lat").reshape(padded, columns)

    rings = lax.axis_size("y")
    second = [(2 * y + 1, 2 * ((y + 1) % rings) + 1) for y in range(rings)]
    turn = innovation[:5]
    for _ in range(3):
        turn = lax.ppermute(turn, ("y", "core"), second)
    vertical = product_vertical(turn, perturb[0], innovation, padded)
    smoothed = meridional(transpose(vertical), bands)
    returned = transpose(smoothed)
    latitude = 1.2 * (lax.axis_index("lat").astype(F32) + 0.5) / bands
    spread = float(max(lon_count // 60, 4)) / jnp.cos(latitude)
    high, low = reach(spread.reshape(1), lon_count // 5, lon_count)
    return zonal(high, low, returned, control[0])[None]


def solution(mesh):
    bands, mem = mesh.shape["lat"], mesh.shape["mem"]
    finer = Mesh(mesh.devices.reshape(bands, mem // 2, 2), ("lat", "y", "core"))
    everything, members = ("lat", "y", "core"), ("y", "core")
    return jax.shard_map(
        local,
        mesh=finer,
        in_specs=(
            P(everything, None),
            P(everything, None),
            P(everything),
            P(everything),
            P("lat", None, members),
            P("lat", None, members),
        ),
        out_specs=P("lat", None, members),
        check_vma=False,
    )
```

```python
import functools

import jax
import jax.numpy as jnp
from jax import lax
from jax.experimental import pallas as pl
from jax.experimental.pallas import tpu as pltpu
from jax.sharding import Mesh, PartitionSpec as P

CAP = 32
F32 = jnp.float32
BF16 = jnp.bfloat16
PARAMS = pltpu.CompilerParams(vmem_limit_bytes=20 * 1024 * 1024)


def split3(x):
    high = x.astype(BF16)
    rest = x - high.astype(F32)
    mid = rest.astype(BF16)
    low = (rest - mid.astype(F32)).astype(BF16)
    return high, mid, low


def split2(x):
    high = x.astype(BF16)
    return high, (x - high.astype(F32)).astype(BF16)


def dot(a, b, dims=((1,), (0,))):
    return lax.dot_general(a, b, (dims, ((), ())), preferred_element_type=F32)


def bucket_kernel(
    rows_any, band_any, cell_any, top_any, out_ref, rows_ref, band_ref, cell_ref, top_ref, sems
):
    levels, count = rows_ref.shape
    bands = out_ref.shape[0] * out_ref.shape[1] // (CAP * levels + 128)
    stride = out_ref.shape[0] // bands
    copies = [
        pltpu.make_async_copy(source, target, sems.at[k])
        for k, (source, target) in enumerate(
            [
                (band_any, band_ref),
                (cell_any, cell_ref),
                (top_any, top_ref),
                (rows_any, rows_ref),
            ]
        )
    ]
    for copy in copies:
        copy.start()
    before = (
        lax.broadcasted_iota(jnp.int32, (count, count), 0)
        < lax.broadcasted_iota(jnp.int32, (count, count), 1)
    ).astype(F32).astype(BF16)
    copies[0].wait()
    owner = (lax.broadcasted_iota(jnp.int32, (bands, count), 0) == band_ref[...]).astype(F32)
    owner_b = owner.astype(BF16)
    earlier = dot(owner_b, before)
    rank = jnp.sum(earlier * owner, axis=0, keepdims=True).astype(jnp.int32)
    for copy in copies[1:]:
        copy.wait()
    kept = lax.broadcasted_iota(jnp.int32, (levels, count), 0) < top_ref[...]
    parts = [part.astype(F32) for part in split3(jnp.where(kept, rows_ref[...], 0.0))]
    for place in range(stride - 1):
        total = None
        for part in parts:
            chosen = jnp.concatenate(
                [jnp.where(rank == 4 * place + k, part, 0.0) for k in range(4)], axis=0
            ).astype(BF16)
            term = dot(owner_b, chosen, ((1,), (1,)))
            total = term if total is None else total + term
        out_ref[pl.ds(place, bands, stride=stride), :] = total
    cells = jnp.where(
        lax.broadcasted_iota(jnp.int32, (128, count), 0) == rank, cell_ref[...].astype(F32), 0.0
    )
    high, low = split2(cells)
    out_ref[pl.ds(stride - 1, bands, stride=stride), :] = dot(
        owner_b, high, ((1,), (1,))
    ) + dot(owner_b, low, ((1,), (1,)))


def bucket(rows, band, cell, top, bands):
    count, levels = rows.shape
    row = pltpu.VMEM((1, count), jnp.int32)
    return pl.pallas_call(
        bucket_kernel,
        out_shape=jax.ShapeDtypeStruct((bands * (CAP * levels // 128 + 1), 128), F32),
        in_specs=[pl.BlockSpec(memory_space=pltpu.HBM)] * 4,
        scratch_shapes=[
            pltpu.VMEM((levels, count), F32),
            row,
            row,
            row,
            pltpu.SemaphoreType.DMA((4,)),
        ],
        compiler_params=PARAMS,
        name="bucket",
    )(
        *(
            pltpu.with_memory_space_constraint(x, pltpu.HBM)
            for x in (
                rows.T,
                band.reshape(1, count),
                cell.reshape(1, count),
                top.reshape(1, count),
            )
        )
    )


def deposit_kernel(got_ref, out_ref, levels):
    groups, per_group, cells = out_ref.shape
    width = 128 // levels
    stride = CAP // width + 1
    sources = got_ref.shape[0] // stride
    spots = got_ref[pl.ds(stride - 1, sources, stride=stride), :]
    acc = jnp.zeros((3 * levels, cells), F32)
    places = lax.broadcasted_iota(jnp.int32, (width * sources, cells), 1).astype(F32)
    for place in range(stride - 1):
        block = jnp.transpose(got_ref[pl.ds(place, sources, stride=stride), :])
        values = jnp.concatenate(
            [block[k * levels : (k + 1) * levels] for k in range(width)], axis=1
        )
        parts = jnp.concatenate(split3(values), axis=0)
        base = place * width
        where = jnp.concatenate([spots[:, base + k : base + k + 1] for k in range(width)], axis=0)
        hits = jnp.where(places == where, 1.0, 0.0).astype(BF16)
        acc = acc + dot(parts, hits)
    grid = acc[:levels] + acc[levels : 2 * levels] + acc[2 * levels :]
    for group in range(groups):
        out_ref[group] = grid[group * per_group : (group + 1) * per_group]


def deposit(got, levels, groups, cells):
    return pl.pallas_call(
        functools.partial(deposit_kernel, levels=levels),
        out_shape=jax.ShapeDtypeStruct((groups, levels // groups, cells), F32),
        compiler_params=PARAMS,
        name="deposit",
    )(got)


def product_kernel(turn_ref, perturb_ref, innovation_ref, out_ref):
    del turn_ref
    cells, columns = perturb_ref.shape
    groups, per_group, _ = innovation_ref.shape
    levels = groups * per_group
    innovation = jnp.concatenate([innovation_ref[g] for g in range(groups)], axis=0)
    parts = jnp.concatenate(split3(innovation), axis=0)
    spread = (
        lax.broadcasted_iota(jnp.int32, (3 * levels, columns), 0) % levels
        == lax.broadcasted_iota(jnp.int32, (3 * levels, columns), 1) % levels
    ).astype(F32).astype(BF16)
    on_columns = dot(parts, spread, ((0,), (0,)))
    product = perturb_ref[...].astype(F32) * on_columns
    row = lax.broadcasted_iota(jnp.int32, (columns, columns), 0)
    column = lax.broadcasted_iota(jnp.int32, (columns, columns), 1)
    distance = (row % levels - column % levels).astype(F32)
    vert = jnp.where(row // levels == column // levels, jnp.exp(-0.5 * distance * distance), 0.0)
    vert_high, vert_low = split2(vert)
    high, low = split2(product)
    out_ref[:cells] = dot(high, vert_high) + (dot(low, vert_high) + dot(high, vert_low))
    out_ref[cells:] = jnp.zeros((out_ref.shape[0] - cells, columns), F32)


def product_vertical(turn, perturb, innovation, rows):
    return pl.pallas_call(
        product_kernel,
        out_shape=jax.ShapeDtypeStruct((rows, perturb.shape[1]), F32),
        compiler_params=PARAMS,
        name="product_vertical",
    )(turn, perturb, innovation)


def meridional_kernel(field_ref, out_ref, bands):
    each = field_ref.shape[0] // bands
    row = lax.broadcasted_iota(jnp.int32, (bands, bands), 0)
    column = lax.broadcasted_iota(jnp.int32, (bands, bands), 1)
    distance = (row - column).astype(F32) / 8.0
    high, low = split2(jnp.exp(-0.5 * distance * distance))
    weights = jnp.concatenate([high, high, low], axis=1)
    for place in range(0, each, 2):
        places = [pl.ds(p, bands, stride=each) for p in range(place, min(place + 2, each))]
        taken = jnp.concatenate([field_ref[rows, :] for rows in places], axis=1)
        field_high, field_low = split2(taken)
        mixed = dot(weights, jnp.concatenate([field_high, field_low, field_high], axis=0))
        for k, rows in enumerate(places):
            out_ref[rows, :] = mixed[:, 128 * k : 128 * (k + 1)]


def meridional(field, bands):
    return pl.pallas_call(
        functools.partial(meridional_kernel, bands=bands),
        out_shape=jax.ShapeDtypeStruct(field.shape, F32),
        compiler_params=PARAMS,
        name="meridional",
    )(field)


def reach_kernel(spread_ref, high_ref, low_ref):
    block, lon_count = high_ref.shape
    place = lax.broadcasted_iota(jnp.int32, (block, lon_count), 0)
    other = lax.broadcasted_iota(jnp.int32, (block, lon_count), 1)
    distance = jnp.abs(place - other).astype(F32)
    distance = jnp.minimum(distance, lon_count - distance) / spread_ref[0]
    high_ref[...], low_ref[...] = split2(jnp.exp(-0.5 * distance * distance))


def reach(spread, block, lon_count):
    part = jax.ShapeDtypeStruct((block, lon_count), BF16)
    return pl.pallas_call(
        reach_kernel,
        out_shape=(part, part),
        in_specs=[pl.BlockSpec(memory_space=pltpu.SMEM)],
        compiler_params=PARAMS,
        cost_estimate=pl.CostEstimate(
            flops=20 * block * lon_count,
            transcendentals=block * lon_count,
            bytes_accessed=4 * block * lon_count,
        ),
        name="reach",
    )(spread)


def zonal_kernel(high_ref, low_ref, field_ref, control_ref, out_ref, twice):
    lon_count, columns = control_ref.shape
    block = high_ref.shape[0]
    high, low = split2(field_ref[:lon_count])
    both = jnp.concatenate([high, low], axis=1)
    twice[0:lon_count] = both
    twice[lon_count : 2 * lon_count] = both
    starts = list(range(0, lon_count, block))
    for pair in range(0, len(starts), 2):
        windows = [twice[first : first + lon_count] for first in starts[pair : pair + 2]]
        narrow = dot(low_ref[...], jnp.concatenate([w[:, :columns] for w in windows], axis=1))
        for k, window in enumerate(windows):
            wide = dot(high_ref[...], window)
            rows = pl.ds(starts[pair + k], block)
            out_ref[rows] = control_ref[rows].astype(F32) + (
                wide[:, :columns]
                + (wide[:, columns:] + narrow[:, k * columns : (k + 1) * columns])
            )


def zonal(high, low, field, control):
    lon_count, columns = control.shape
    return pl.pallas_call(
        zonal_kernel,
        out_shape=jax.ShapeDtypeStruct(control.shape, F32),
        scratch_shapes=[pltpu.VMEM((2 * lon_count, 2 * columns), BF16)],
        compiler_params=PARAMS,
        name="zonal",
    )(high, low, field, control)


def local(obs_rows, obs_band, obs_cell, obs_top, perturb, control):
    bands = lax.axis_size("lat")
    mem = lax.axis_size("core") * lax.axis_size("y")
    _, lon_count, columns = perturb.shape
    levels = obs_rows.shape[1]

    def exchange(pieces, axes):
        return lax.all_to_all(pieces, axes, split_axis=0, concat_axis=0, tiled=True)

    send = bucket(obs_rows, obs_band, obs_cell, obs_top, bands)
    got = exchange(send.reshape(bands, 1, -1), "lat").reshape(send.shape)
    pieces = exchange(deposit(got, levels, mem, lon_count), ("core", "y"))
    piece = jnp.sum(pieces, axis=0, keepdims=True)
    innovation = exchange(jnp.broadcast_to(piece, pieces.shape), ("core", "y"))
    each = -(-lon_count // bands)
    padded = each * bands

    def transpose(field):
        pieces = field.reshape(bands, 1, each * columns)
        return exchange(pieces, "lat").reshape(padded, columns)

    rings = lax.axis_size("y")
    second = [(2 * y + 1, 2 * ((y + 1) % rings) + 1) for y in range(rings)]
    turn = innovation[:6]
    for _ in range(3):
        turn = lax.ppermute(turn, ("y", "core"), second)
    vertical = product_vertical(turn, perturb[0], innovation, padded)
    smoothed = meridional(transpose(vertical), bands)
    returned = transpose(smoothed)
    latitude = 1.2 * (lax.axis_index("lat").astype(F32) + 0.5) / bands
    spread = float(max(lon_count // 60, 4)) / jnp.cos(latitude)
    high, low = reach(spread.reshape(1), lon_count // 5, lon_count)
    return zonal(high, low, returned, control[0])[None]


def solution(mesh):
    bands, mem = mesh.shape["lat"], mesh.shape["mem"]
    finer = Mesh(mesh.devices.reshape(bands, mem // 2, 2), ("lat", "y", "core"))
    everything, members = ("lat", "y", "core"), ("y", "core")
    return jax.shard_map(
        local,
        mesh=finer,
        in_specs=(
            P(everything, None),
            P(everything, None),
            P(everything),
            P(everything),
            P("lat", None, members),
            P("lat", None, members),
        ),
        out_specs=P("lat", None, members),
        check_vma=False,
    )
```
